32 devices in a mesh: batch: 8 (over z, x), chan: 4 (over y, core).
Axes of the slice: x: 2, y: 2, z: 4, core: 2. Of those that a mesh axis runs over, the one named last changes fastest.
Arguments:
- signal: float32 [1024, 32768], P('chan', 'batch'), may hold values from -6 to 6
- cotangent: float32 [1024, 32768], P('chan', 'batch'), may hold values from -6 to 6
- first_layer: float32 [33, 64], replicated, may hold values from -5 to 5
- second_layer: float32 [64, 1024], P(None, 'chan'), may hold values from -0.75 to 0.75
- decay_rate: float32 [1024], P('chan'), may hold values from 0.3 to 600
- skip_gain: float32 [1024], P('chan'), may hold values from -4 to 4
Outputs:
- input_grad: float32 [1024, 32768], P('chan', 'batch')
- first_grad: float32 [33, 64], replicated
- second_grad: float32 [64, 1024], P(None, 'chan')
- decay_grad: float32 [1024], P('chan')
- skip_grad: float32 [1024], P('chan')
The draws below stay inside these ranges and needn't reach their ends.
All inputs are finite; a program needn't handle non-finite values.
Results may differ from the reference program's by a relative error of at most 0.0003.
Values sent between devices are 32-bit elements; how exact they have to be, the bound alone decides.
A program may use at most 256 MiB of HBM per device.

```python
import math
import jax
import jax.numpy as jnp
from jax import lax

WIDTH = 1024
LENGTH = 32768
ORDER = 64
BANDS = 16
EMBED = 33


def block_levels(key, shape, pieces, smallest, top_value):
    gain, own = 1.0, jax.random.fold_in(key, 6)
    for position, parts in pieces:
        heights = jnp.exp(jax.random.uniform(jax.random.fold_in(own, position), (parts,), jnp.float32, smallest / len(pieces), top_value / len(pieces)))
        gain = gain * jnp.repeat(heights, shape[position] // parts).reshape([-1 if axis == position else 1 for axis in range(len(shape))])
    return gain


def scatter_about(own_key, extent, deviation, reach, split=(), kind=jnp.bfloat16):
    result = deviation * jax.random.normal(own_key, extent, jnp.float32)
    if split:
        result = result * block_levels(own_key, extent, split, -0.22, 0.18)
    return jnp.clip(result, -reach, reach).astype(kind)


def setup_inputs(seed: int = 0) -> dict:
    key_of = jax.random.split(jax.random.key(seed), 7)
    return {
        "signal": scatter_about(key_of[0], (WIDTH, LENGTH), 1.0, 6.0, ((0, 4), (1, 8)), jnp.float32),
        "cotangent": scatter_about(key_of[1], (WIDTH, LENGTH), 1.0, 6.0, ((0, 4), (1, 8)), jnp.float32),
        "first_layer": scatter_about(key_of[2], (EMBED, ORDER), 1.0, 5.0, (), jnp.float32),
        "second_layer": scatter_about(key_of[3], (ORDER, WIDTH), ORDER ** -0.5, 0.75, ((1, 4),), jnp.float32),
        "decay_rate": jnp.clip(jnp.exp(math.log(600.0) - 7.6009024 * jax.random.uniform(key_of[4], (WIDTH,), jnp.float32) ** block_levels(key_of[4], (WIDTH,), ((0, 4),), -0.2, 0.2)), 0.3, 600.0),
        "skip_gain": scatter_about(key_of[5], (WIDTH,), 1.0, 4.0, ((0, 4),), jnp.float32),
    }


precise = lax.Precision.HIGHEST
epsilon = 1e-06

def features(positions, length, band_count):
    band_index = jnp.arange(1, band_count + 1, dtype=jnp.int32)
    phase = (band_index[:, None] * positions[None, :] % length).astype(jnp.float32) * (2.0 * math.pi / length)
    linear = positions.astype(jnp.float32)[None, :] / length
    return jnp.concatenate([linear, jnp.cos(phase), jnp.sin(phase)], axis=0)

def reference(signal, cotangent, first_layer, second_layer, decay_rate, skip_gain):
    positions = jnp.arange(LENGTH, dtype=jnp.int32)
    embed = features(positions, LENGTH, BANDS)
    before = jnp.dot(first_layer.T, embed, precision=precise)
    basis = jnp.sin(before)
    fraction = positions.astype(jnp.float32) / LENGTH
    factor = 1.0 / math.sqrt(LENGTH)
    padded = 2 * LENGTH
    stride = 64
    blocks_count = WIDTH // stride

    def step(carry, index):
        start = (index * stride).astype(jnp.int32)
        values = lax.dynamic_slice_in_dim(signal, start, stride, 0)
        cotan = lax.dynamic_slice_in_dim(cotangent, start, stride, 0)
        columns = lax.dynamic_slice_in_dim(second_layer, start, stride, 1)
        rates = lax.dynamic_slice_in_dim(decay_rate, start, stride, 0)
        gains = lax.dynamic_slice_in_dim(skip_gain, start, stride, 0)
        window = jnp.exp(-rates[:, None] * fraction[None, :])
        shaped = window * jnp.dot(columns.T, basis, precision=precise)
        norms = jnp.sqrt(lax.optimization_barrier(jnp.sum(shaped * shaped, axis=1, keepdims=True)) + epsilon)
        filt = shaped / norms
        spec_val = jnp.fft.rfft(values, n=padded)
        spec_cot = jnp.fft.rfft(cotan, n=padded)
        spec_filt = jnp.fft.rfft(filt, n=padded)
        in_grad = jnp.fft.irfft(jnp.conj(spec_filt) * spec_cot, n=padded)[:, :LENGTH] + gains[:, None] * cotan
        dfilt = factor * jnp.fft.irfft(jnp.conj(spec_val) * spec_cot, n=padded)[:, :LENGTH]
        skip_part = factor * lax.optimization_barrier(jnp.sum(cotan * values, axis=1))
        project = lax.optimization_barrier(jnp.sum(filt * dfilt, axis=1, keepdims=True))
        draw = (dfilt - filt * project) / norms
        decay_part = -lax.optimization_barrier(jnp.sum(draw * shaped * fraction[None, :], axis=1))
        dmix = draw * window
        second_part = jnp.dot(basis, dmix.T, precision=precise)
        carry = carry + jnp.dot(columns, dmix, precision=precise)
        return (carry, (in_grad.astype(jnp.float32), second_part, decay_part, skip_part))
    dbasis, results = lax.scan(step, jnp.zeros((ORDER, LENGTH), jnp.float32), jnp.arange(blocks_count, dtype=jnp.int32))
    in_blocks, second_blocks, decay_blocks, skip_blocks = results
    input_grad = in_blocks.reshape(WIDTH, LENGTH)
    second_grad = jnp.transpose(second_blocks, (1, 0, 2)).reshape(ORDER, WIDTH)
    decay_grad = decay_blocks.reshape(WIDTH)
    skip_grad = skip_blocks.reshape(WIDTH)
    first_grad = jnp.dot(embed, (jnp.cos(before) * dbasis).T, precision=precise)
    return (input_grad, first_grad, second_grad, decay_grad, skip_grad)
```

```python
import functools
import math

import jax
import jax.numpy as jnp
import numpy as np
from jax import lax
from jax.experimental import pallas as pl
from jax.experimental.pallas import tpu as pltpu
from jax.sharding import PartitionSpec as P

COLS = 256

exact = lax.Precision.HIGHEST
precise = lax.Precision.HIGH
epsilon = 1e-06


def sincos(x):
    turns = jnp.round(x * (2.0 / math.pi))
    r = x - turns * 1.5703125
    r = r - turns * 4.837512969970703125e-4
    r = r - turns * 7.549789948768648e-8
    sq = r * r
    sine = r + r * sq * (-1.6666654611e-1 + sq * (8.3321608736e-3 + sq * -1.9515295891e-4))
    cosine = 1.0 - 0.5 * sq + sq * sq * (
        4.166664568298827e-2 + sq * (-1.388731625493765e-3 + sq * 2.443315711809948e-5)
    )
    quadrant = turns.astype(jnp.int32) & 3
    odd = (quadrant & 1) == 1
    sin_value = jnp.where(odd, cosine, sine)
    cos_value = jnp.where(odd, sine, cosine)
    sin_value = jnp.where(quadrant >= 2, -sin_value, sin_value)
    cos_value = jnp.where((quadrant == 1) | (quadrant == 2), -cos_value, cos_value)
    return sin_value, cos_value


def features(positions, length, band_count):
    band_index = jnp.arange(1, band_count + 1, dtype=jnp.int32)
    phase = (band_index[:, None] * positions[None, :] % length).astype(jnp.float32) * (
        2.0 * math.pi / length
    )
    linear = positions.astype(jnp.float32)[None, :] / length
    sines, cosines = sincos(phase)
    return jnp.concatenate([linear, cosines, sines], axis=0)


def pair(matrix):
    high = matrix.astype(np.float32).astype(jnp.bfloat16)
    low = (matrix - high.astype(np.float64)).astype(np.float32).astype(jnp.bfloat16)
    return jnp.asarray(high), jnp.asarray(low)


def tables(rows, cols):
    r = np.arange(rows, dtype=np.float64)
    c = np.arange(cols, dtype=np.float64)
    first = 2.0 * np.pi * np.outer(r + 0.5, r) / (2 * rows)
    twist = 2.0 * np.pi * np.outer(r + 0.5, c) / (2 * rows * cols)
    angle = 2.0 * np.pi * (np.outer(c, c) % cols) / cols
    cos_c, sin_c = np.cos(angle), np.sin(angle)
    stage1 = np.concatenate([np.cos(first), -np.sin(first)], axis=0)
    stage2 = np.block([[cos_c, -sin_c], [sin_c, cos_c]])
    last = np.concatenate([np.cos(first.T), -np.sin(first.T)], axis=1) / (rows * cols)
    return (
        *pair(stage1),
        *pair(stage2),
        *pair(stage2.T.copy()),
        *pair(last),
        jnp.asarray(np.cos(twist), jnp.float32),
        jnp.asarray(np.sin(twist), jnp.float32),
    )


def split(x):
    high = x.astype(jnp.bfloat16)
    return high, (x - high.astype(jnp.float32)).astype(jnp.bfloat16)


def dot(a, b):
    return jnp.dot(a, b, preferred_element_type=jnp.float32)


def product(left, right):
    return dot(left[0], right[0]) + (dot(left[1], right[0]) + dot(left[0], right[1]))


def kernel(count, val, cot, filt, w1h, w1l, w2h, w2l, w3h, w3l, w4h, w4l, ct, st, out_in, out_filt):
    rows, cols = ct.shape
    cos_t, sin_t = ct[...], st[...]
    first = (w1h[...], w1l[...])
    for c in range(count):
        parts = []
        for ref in (val, cot, filt):
            t = product(first, split(ref[c]))
            re, im = t[:rows], t[rows:]
            parts.append(
                jnp.concatenate([re * cos_t + im * sin_t, im * cos_t - re * sin_t], axis=1)
            )
        spec = product(split(jnp.concatenate(parts, axis=0)), (w2h[...], w2l[...]))
        v_re, v_im = spec[:rows, :cols], spec[:rows, cols:]
        c_re, c_im = spec[rows : 2 * rows, :cols], spec[rows : 2 * rows, cols:]
        f_re, f_im = spec[2 * rows :, :cols], spec[2 * rows :, cols:]
        prods = jnp.concatenate(
            [
                jnp.concatenate([f_re * c_re + f_im * c_im, f_re * c_im - f_im * c_re], axis=1),
                jnp.concatenate([v_re * c_re + v_im * c_im, v_re * c_im - v_im * c_re], axis=1),
            ],
            axis=0,
        )
        back = product(split(prods), (w3h[...], w3l[...]))
        for i, out in enumerate((out_in, out_filt)):
            re, im = back[i * rows : (i + 1) * rows, :cols], back[i * rows : (i + 1) * rows, cols:]
            turn = jnp.concatenate([re * cos_t - im * sin_t, im * cos_t + re * sin_t], axis=0)
            out[c] = product((w4h[...], w4l[...]), split(turn))


def correlate(values, cotan, filt):
    channels, rows, cols = values.shape
    count = 2 if channels % 2 == 0 else 1
    tabs = tables(rows, cols)
    block = pl.BlockSpec((count, rows, cols), lambda i: (i, 0, 0))
    shape = jax.ShapeDtypeStruct(values.shape, jnp.float32)
    flops = 2 * 3 * channels * rows * cols * (5 * 2 * rows + 5 * 4 * cols)
    return pl.pallas_call(
        functools.partial(kernel, count),
        grid=(channels // count,),
        in_specs=[block] * 3 + [pl.BlockSpec(t.shape, lambda i: (0, 0)) for t in tabs],
        out_specs=[block, block],
        out_shape=[shape, shape],
        compiler_params=pltpu.CompilerParams(vmem_limit_bytes=56 * 1024 * 1024),
        cost_estimate=pl.CostEstimate(
            flops=flops, bytes_accessed=5 * 4 * values.size, transcendentals=0
        ),
        name="correlate",
    )(values, cotan, filt, *tabs)


def local(signal, cotangent, first_layer, second_layer, decay_rate, skip_gain):
    groups = lax.axis_size("batch")
    place = lax.axis_index("batch")
    width_dev, local_len = signal.shape
    length = local_len * groups
    cols = COLS
    factor = 1.0 / math.sqrt(length)
    narrow = width_dev // groups

    def spread(x):
        x = x.reshape(width_dev, local_len // cols, cols)
        return lax.all_to_all(x, "batch", split_axis=0, concat_axis=1, tiled=True)

    val, cot = spread(signal), spread(cotangent)
    positions = jnp.arange(length, dtype=jnp.int32)
    columns = lax.dynamic_slice_in_dim(second_layer, place * narrow, narrow, 1)
    rates = lax.dynamic_slice_in_dim(decay_rate, place * narrow, narrow, 0)
    gains = lax.dynamic_slice_in_dim(skip_gain, place * narrow, narrow, 0)
    embed = features(positions, length, first_layer.shape[0] // 2)
    before = jnp.dot(first_layer.T, embed, precision=exact)
    basis, slope = sincos(before)
    fraction = positions.astype(jnp.float32) / length
    window = jnp.exp(-rates[:, None] * fraction[None, :])
    shaped = window * jnp.dot(columns.T, basis, precision=precise)
    norms = jnp.sqrt(jnp.sum(shaped * shaped, axis=1, keepdims=True) + epsilon)
    filt = shaped / norms
    taps = filt + jnp.where(positions[None, :] == 0, gains[:, None], 0.0)
    in_grad, filt_grad = correlate(val, cot, taps.reshape(val.shape))
    input_grad = lax.all_to_all(in_grad, "batch", split_axis=1, concat_axis=0, tiled=True)
    input_grad = input_grad.reshape(width_dev, local_len)
    dfilt = factor * filt_grad.reshape(narrow, length)
    skip_part = factor * jnp.sum(cot * val, axis=(1, 2))
    project = jnp.sum(filt * dfilt, axis=1, keepdims=True)
    draw = (dfilt - filt * project) / norms
    decay_part = -jnp.sum(draw * shaped * fraction[None, :], axis=1)
    dmix = draw * window
    second_part = jnp.dot(basis, dmix.T, precision=precise)
    dbasis = jnp.dot(columns, dmix, precision=precise)
    first_part = jnp.dot(embed, (slope * dbasis).T, precision=precise)
    second_grad, decay_grad, skip_grad = (
        lax.all_gather(second_part, "batch", axis=1, tiled=True),
        lax.all_gather(decay_part, "batch", axis=0, tiled=True),
        lax.all_gather(skip_part, "batch", axis=0, tiled=True),
    )
    first_grad = lax.psum(first_part, ("batch", "chan"))
    return (input_grad, first_grad, second_grad, decay_grad, skip_grad)


def solution(mesh):
    placed = (P("chan", "batch"), P("chan", "batch"), P(), P(None, "chan"), P("chan"), P("chan"))
    return jax.shard_map(
        local,
        mesh=mesh,
        in_specs=placed,
        out_specs=(P("chan", "batch"), P(), P(None, "chan"), P("chan"), P("chan")),
        check_vma=False,
    )
```
